512 devices in a mesh: dp: 16 (over y, x), expert: 32 (over z, core).
Axes of the slice: x: 4, y: 4, z: 16, core: 2. Of those that a mesh axis runs over, the one named last changes fastest.
Arguments:
- cotangent: bfloat16 [65536, 4096], P(('dp', 'expert')), may hold values from -0.59765625 to 0.59765625
- expert_ids: int32 [65536, 8], P(('dp', 'expert')), may hold values from 0 to 63, all different within a row; in each aligned block of 128 rows (0 to 127, 128 to 255, ...) at most 20 rows name the same one
- gates: bfloat16 [65536, 8], P(('dp', 'expert')), may hold values from 0.019897461 to 0.5
- hidden: bfloat16 [64, 16, 640, 1536], P('expert', 'dp'), may hold values from -6 to 6
- q_prev: bfloat16 [64, 4096, 64], P('expert', 'dp'), may hold values from -0.09375 to 0.09375
Outputs:
- p_merged: float32 [64, 1536, 64], P('expert', 'dp')
- q_next: float32 [64, 4096, 64], P('expert', 'dp')
The draws below stay inside these ranges and needn't reach their ends.
Inputs may be any that keep to these rules, and one draw needn't show every extreme that they name: `expert_ids`: each row names 8 different experts. Within the 128 rows of one device no expert is named by more than 20 rows, a bound that some block reaches.
All inputs are finite; a program needn't handle non-finite values.
Results may differ from the reference program's by a relative error of at most 0.0056.
Values may be sent and summed in bfloat16 or wider, within the bound.
A program may use at most 128 MiB of HBM per device.

```python
import math
import jax
import jax.numpy as jnp
import numpy as np
from jax import lax

D = 4096
FF = 1536
TOP = 8
RANK = 64
TOK_DEV = 128
EXPERTS = 64
CAP = 20
SLOTS = 640
TOKENS = 65536
N_DP = 16
N_EXPERT = 32


def block_scale(own_key, shape, split, least, high):
    gain, own = 1.0, jax.random.fold_in(own_key, 6)
    for dim, shards_of in split:
        heights = jnp.exp(jax.random.uniform(jax.random.fold_in(own, dim), (shards_of,), jnp.float32, least / len(split), high / len(split)))
        gain = gain * jnp.repeat(heights, shape[dim] // shards_of).reshape([-1 if axis == dim else 1 for axis in range(len(shape))])
    return gain


def assign_block(stream_key, own, number, rows, count, top, reach, lean):
    sequence = jax.random.permutation(stream_key, count)
    heavy_load, usual = portions_of(count, rows * top, reach, lean, True), portions_of(count, rows * top, reach, lean, False)
    places = jnp.arange(count)

    def named(sizes, offset_by):
        used = int((sizes > 0).sum())
        fixed = max(1, used // 4)
        moved = fixed + (places - fixed + offset_by * (used - fixed)) % max(1, count - fixed)
        return jnp.zeros((count,), jnp.int32).at[sequence[jnp.where(places < fixed, places, moved)]].set(jnp.asarray(sizes, jnp.int32))

    sizes = jnp.where(number % 4 == 0, named(heavy_load, number // 4), named(usual, number - number // 4 - 1))
    mixed = jax.random.permutation(jax.random.fold_in(own, 3), count)
    donor, sink = mixed[0:count // 2 * 2:2], mixed[1:count // 2 * 2:2]
    room = jnp.minimum(sizes[donor] - 1, reach - sizes[sink]) // 2
    room = jnp.where((donor == sequence[0]) | (sink == sequence[0]) | (sizes[sink] == 0), 0, jnp.maximum(room, 0))
    moved = jax.random.randint(jax.random.fold_in(own, 4), (count // 2,), 0, 1 << 20) % (room + 1)
    sizes = sizes.at[donor].add(-moved).at[sink].add(moved)
    members = jnp.searchsorted(jnp.cumsum(sizes), jnp.arange(rows * top), side="right").astype(jnp.int32)
    grid = members.reshape(top, rows).T
    grid = grid[jax.random.permutation(jax.random.fold_in(own, 1), rows)]
    offset_by = jax.random.randint(jax.random.fold_in(own, 2), (rows, 1), 0, top)
    return jnp.take_along_axis(grid, (jnp.arange(top)[None, :] + offset_by) % top, axis=1)


def portions_of(number_of, total, reach, skew, full):
    portions = [(1 << 20) // math.isqrt(grade ** skew) + 1 for grade in range(1, number_of + 1)]
    largest = reach if full else min(reach, max(-(-total // number_of), total * portions[0] // sum(portions)))
    least = 1 if total - largest >= number_of - 1 else 0
    counts, spare = [largest] + [least] * (number_of - 1), total - largest - least * (number_of - 1)
    while spare > 0:
        candidates = [i for i in range(1, number_of) if counts[i] < largest] or [i for i in range(1, number_of) if counts[i] < reach]
        whole, remaining = sum([portions[i] for i in candidates]), spare
        for i in candidates:
            extra = min(reach - counts[i], max(1, remaining * portions[i] // whole), spare)
            counts[i] = counts[i] + extra
            spare = spare - extra
    return np.array(counts)


def normal_values(stream_key, dims, scale, limit, pieces=(), kind=jnp.bfloat16):
    result = scale * jax.random.normal(stream_key, dims, jnp.float32)
    if pieces:
        result = result * block_scale(stream_key, dims, pieces, -0.22, 0.18)
    return jnp.clip(result, -limit, limit).astype(kind)


def setup_inputs(seed: int = 0) -> dict:
    key_of = jax.random.split(jax.random.key(seed), 6)
    cotangent = normal_values(key_of[0], (TOKENS, D), 0.1, 0.59765625, ((0, 512),))
    expert_ids_keys = jax.random.split(jax.random.fold_in(key_of[1], 1), TOKENS // TOK_DEV)
    expert_ids_turns = jax.random.permutation(jax.random.fold_in(key_of[1], 3), TOKENS // TOK_DEV)
    expert_ids = jax.vmap(lambda own, number: assign_block(jax.random.fold_in(key_of[1], 2), own, number, TOK_DEV, EXPERTS, TOP, CAP, 2))(expert_ids_keys, expert_ids_turns).reshape((TOKENS, TOP))
    gates = jnp.clip(jnp.exp(math.log(0.5) - 3.224016 * jax.random.uniform(key_of[2], (TOKENS, TOP), jnp.float32) ** block_scale(key_of[2], (TOKENS, TOP), ((0, 512),), -0.2, 0.2)), 0.019897461, 0.5).astype(jnp.bfloat16)
    hidden = normal_values(key_of[3], (EXPERTS, N_DP, SLOTS, FF), 1.0, 6.0, ((0, 32), (1, 16)))
    q_prev = normal_values(key_of[4], (EXPERTS, D, RANK), D ** -0.5, 0.09375, ((0, 32), (1, 16)))
    return {"cotangent": cotangent, "expert_ids": expert_ids, "gates": gates, "hidden": hidden, "q_prev": q_prev}


def reference(cotangent, expert_ids, gates, hidden, q_prev):
    blocks = N_DP * N_EXPERT
    per_block = TOK_DEV * TOP
    block_ids = expert_ids.reshape(blocks, per_block)
    labels = jnp.arange(EXPERTS, dtype=jnp.int32)
    onehot = (block_ids[:, :, None] == labels[None, None, :]).astype(jnp.int32)
    earlier = jnp.cumsum(onehot, axis=1) - onehot
    slot_index = jnp.sum(earlier * onehot, axis=2).astype(jnp.int32)
    block_index = jnp.arange(blocks, dtype=jnp.int32)[:, None]
    token_index = block_index * TOK_DEV + jnp.arange(per_block, dtype=jnp.int32)[None, :] // TOP
    row_key = (block_ids * (blocks * CAP) + block_index * CAP + slot_index).reshape(-1)
    row_total = EXPERTS * blocks * CAP
    token_rows = jnp.zeros((row_total,), jnp.int32).at[row_key].set(token_index.reshape(-1).astype(jnp.int32))
    gate_rows = jnp.zeros((row_total,), jnp.float32).at[row_key].set(gates.reshape(-1).astype(jnp.float32))
    token_rows = token_rows.reshape(EXPERTS, blocks * CAP)
    gate_rows = gate_rows.reshape(EXPERTS, blocks * CAP)

    def one_expert(expert_items):
        token_part, gate_part, hidden_part, factor = expert_items
        dispatched = (gate_part[:, None] * cotangent[token_part].astype(jnp.float32)).astype(jnp.bfloat16)
        projected = jnp.dot(dispatched.astype(jnp.float32), factor.astype(jnp.float32), preferred_element_type=jnp.float32).astype(jnp.bfloat16)
        hidden_rows = hidden_part.reshape(blocks * CAP, FF)
        merged = jnp.dot(hidden_rows.T.astype(jnp.float32), projected.astype(jnp.float32), preferred_element_type=jnp.float32)
        gram_matrix = jnp.dot(merged.T, merged, precision=lax.Precision.HIGHEST)
        lower_factor = jnp.linalg.cholesky(gram_matrix)
        solved = jax.scipy.linalg.solve_triangular(lower_factor, merged.T, lower=True)
        basis_rows = solved.T.astype(jnp.bfloat16)
        mapped = jnp.dot(hidden_rows.astype(jnp.float32), basis_rows.astype(jnp.float32), preferred_element_type=jnp.float32).astype(jnp.bfloat16)
        q_summed = jnp.dot(dispatched.T.astype(jnp.float32), mapped.astype(jnp.float32), preferred_element_type=jnp.float32)
        return (merged, q_summed)
    p_merged, q_next = lax.map(one_expert, (token_rows, gate_rows, hidden, q_prev))
    return (p_merged, q_next)
```

```python
import functools

import jax
import jax.numpy as jnp
from jax import lax
from jax.experimental import pallas as pl
from jax.experimental.pallas import tpu as pltpu
from jax.sharding import PartitionSpec as P

F32, BF16 = jnp.float32, jnp.bfloat16
MESH = pl.DeviceIdType.MESH
NT = (((1,), (1,)), ((), ()))
TN = (((0,), (0,)), ((), ()))
LANES = 128
SLOT_ROWS = 32
UNIT_GROUP = 2
RING_EVERY = 3


def rdma(src, dst, send_sem, recv_sem, device):
    return pltpu.make_async_remote_copy(
        src_ref=src, dst_ref=dst, send_sem=send_sem, recv_sem=recv_sem,
        device_id=device, device_id_type=MESH,
    )


def iota(shape, dim):
    return lax.broadcasted_iota(jnp.int32, shape, dim)


def steps(start, stop, body):
    def run(i, carry):
        body(i)
        return carry

    lax.fori_loop(start, stop, run, 0)


def whitening(gram):
    half = gram.shape[0] // 2
    lane, row = iota((half, LANES), 1), iota((half, LANES), 0)
    low = lane < half
    eye = jnp.where((lane == row) | (lane == row + half), 1.0, 0.0).astype(F32)
    tables = [jnp.where(low, gram[:half], eye), jnp.where(low, eye, gram[half:])]
    blocks = [[t[8 * b : 8 * b + 8] for b in range(half // 8)] for t in tables]
    sub = iota((8, LANES), 0)
    for k in range(half):
        own, at = k // 8, k % 8
        for which in range(2):
            parts = blocks[which]
            pivot_lane = k + which * half
            pivot_row = parts[own][at : at + 1, :]
            scaled = pivot_row / pivot_row[:, pivot_lane : pivot_lane + 1]
            for b in range(own, half // 8):
                column = parts[b][:, pivot_lane : pivot_lane + 1]
                update = column * scaled
                if b == own:
                    update = jnp.where(sub > at, update, 0.0)
                parts[b] = parts[b] - update
    done = [jnp.concatenate(parts, axis=0) for parts in blocks]
    result = []
    for which in range(2):
        diag = jnp.sum(
            jnp.where(lane == row + which * half, done[which], 0.0), axis=1, keepdims=True
        )
        moved = pltpu.roll(done[which] * lax.rsqrt(diag), half, 1)
        result.append(jnp.where(low if which == 0 else jnp.logical_not(low), moved, 0.0))
    return jnp.concatenate(result, axis=0)


def kernel(
    dims,
    cot, ids, gts, qt, hid,
    p_out, q_out,
    cotb, gb, rmat, cmat, emat, etmat, disp, qb, sbuf, rb, zs, pz, hv, p640,
    ptp, prb, pfull, btr, zs2, mz, mg, ybuf, qp, qh, fs, fr, bs, br,
    hsem, s_cot, r_cot, s_g, r_g, s_q, r_q, s_qp, r_qp, s_rs, r_rs, s_z, r_z,
    s_p, r_p, s_pf, r_pf, s_m, r_m, s_mg, r_mg, s_h, r_h, s_f, r_f, s_b, r_b,
):
    G, J, cap = dims
    Z, U = J // 2, J // 4
    V = max(1, U // UNIT_GROUP)
    UG = U // V
    T, width = cot.shape
    Dd = width // G
    unit = 4 * cap
    half = 2 * cap
    GB = min(4, G)
    R8 = LANES // G
    FF = hid.shape[-1]
    g = lax.axis_index("dp")
    j = lax.axis_index("expert")
    z, c = lax.div(j, 2), lax.rem(j, 2)
    mate = j + 1 - 2 * c
    up = lax.rem(z + 1, Z) * 2 + c
    down = lax.rem(z + Z - 1, Z) * 2 + c

    def dp(k):
        return lax.rem(g + k, G)

    def chip(m):
        return lax.rem(z + ((m + 1) // 2 if m % 2 else Z - m // 2), Z)

    hcopy = pltpu.make_async_copy(hid.at[:, 0], hv, hsem)
    hcopy.start()

    barrier = pltpu.get_barrier_semaphore()

    def greet_dp(k):
        pl.semaphore_signal(barrier, inc=1, device_id={"dp": dp(k)}, device_id_type=MESH)

    def greet_expert(k):
        pl.semaphore_signal(
            barrier, inc=1, device_id={"expert": lax.rem(j + k, J)}, device_id_type=MESH
        )

    steps(1, G, greet_dp)
    steps(1, J, greet_expert)

    lane_t = iota((T, LANES), 1)
    gate = jnp.zeros((T, LANES), F32)
    named = jnp.zeros((T, LANES), F32)
    for k in range(ids.shape[1]):
        one = ids[:, k : k + 1]
        gate = gate + jnp.where(lane_t == one, gts[:, k : k + 1].astype(F32), 0.0)
        named = named + jnp.where(lane_t == one + 64, 1.0, 0.0)
    earlier = jnp.where(iota((T, T), 1) < iota((T, T), 0), 1.0, 0.0).astype(BF16)
    slots = jnp.dot(earlier, named.astype(BF16), preferred_element_type=F32)
    gb[g] = jnp.where(lane_t < 64, gate, slots).astype(BF16)

    r80, l80 = iota((unit, LANES), 0), iota((unit, LANES), 1)
    core80 = jnp.where((r80 >= cap) & (r80 < half), 1, 0) + jnp.where(r80 >= half + cap, 1, 0)
    h80 = jnp.where(r80 >= half, 1, 0)
    base80 = 2 * core80 + h80
    slot80 = r80 - cap * core80 - half * h80
    for i in range(4):
        cmat[unit * i : unit * (i + 1), :] = slot80.astype(F32)
    for m in range(Z):
        rmat[unit * m : unit * (m + 1), :] = jnp.where(
            l80 == base80 + 4 * chip(m), 1.0, 0.0
        ).astype(BF16)
    er, el = iota((LANES, LANES), 0), iota((LANES, LANES), 1)
    eblk = (
        jnp.where(er >= SLOT_ROWS, 1, 0)
        + jnp.where(er >= 2 * SLOT_ROWS, 1, 0)
        + jnp.where(er >= 3 * SLOT_ROWS, 1, 0)
    )
    inside = er - SLOT_ROWS * eblk
    emat[...] = jnp.where((inside < cap) & (el == inside + cap * eblk), 1.0, 0.0).astype(BF16)
    tblk = (
        jnp.where(r80 >= cap, 1, 0)
        + jnp.where(r80 >= 2 * cap, 1, 0)
        + jnp.where(r80 >= 3 * cap, 1, 0)
    )
    etmat[...] = jnp.where(l80 == r80 + (SLOT_ROWS - cap) * tblk, 1.0, 0.0).astype(BF16)

    pl.semaphore_wait(barrier, G + J - 2)

    def cot_copy(k):
        d = dp(k)
        return rdma(
            cot.at[:, pl.ds(pl.multiple_of(d * Dd, Dd), Dd)], cotb.at[g],
            s_cot.at[k], r_cot.at[g], {"dp": d},
        )

    def g_copy(k):
        return rdma(gb.at[g], gb.at[g], s_g.at[k], r_g.at[g], {"dp": dp(k)})

    def ring_copy(src, m, sem_at, device):
        return rdma(src, qb.at[m, c], s_q.at[sem_at], r_q.at[m], {"expert": device})

    def mate_copy(src, m):
        return rdma(src, qb.at[m, c], s_qp.at[m], r_qp.at[m], {"expert": mate})

    def ring_first():
        ring_copy(qt, 1, 1, down).start()
        if Z > 2:
            ring_copy(qt, 2, 2, up).start()
        mate_copy(qt, 0).start()

    ring_first()

    def send_cot(k):
        g_copy(k).start()
        cot_copy(k).start()

    steps(1, G, send_cot)
    qb[0, c] = qt[...]
    cotb[g] = cot[:, pl.ds(pl.multiple_of(g * Dd, Dd), Dd)]

    def ring_step(s):
        m = 2 * s - 1
        ring_copy(qb.at[m, c], m, m, down).wait_recv()

        @pl.when(s < Z // 2)
        def _():
            ring_copy(qb.at[m, c], m + 2, m + 2, down).start()

        mate_copy(qb.at[m, c], m).start()

        @pl.when(s < Z // 2)
        def _():
            n = 2 * s
            ring_copy(qb.at[n, c], n, n, up).wait_recv()

            @pl.when(s < Z // 2 - 1)
            def _():
                ring_copy(qb.at[n, c], n + 2, n + 2, up).start()

            mate_copy(qb.at[n, c], n).start()

    early = min((G - 1) // RING_EVERY, Z // 2)
    QC = min(4, Z)
    rows_q = unit * QC

    def dispatch_step(k):
        src = lax.rem(g + G - k, G)

        @pl.when(k > 0)
        def _():
            rdma(gb.at[src], gb.at[src], s_g.at[k], r_g.at[src], {"dp": src}).wait_recv()
            rdma(cotb.at[src], cotb.at[src], s_cot.at[k], r_cot.at[src], {"dp": src}).wait_recv()

        table = gb[src].astype(F32)
        both = jnp.concatenate([table, pltpu.roll(table, 64, 1)], axis=0).astype(BF16)
        tokens = cotb[src]

        def block(i):
            at = pl.multiple_of(i * rows_q, rows_q)
            spread = lax.dot_general(
                rmat[pl.ds(at, rows_q), :], both, NT, preferred_element_type=F32
            )
            hit = spread[:, T:] == cmat[:rows_q, :]
            chooser = jnp.where(hit, spread[:, :T], 0.0).astype(BF16)
            rows = jnp.dot(chooser, tokens, preferred_element_type=F32).astype(BF16)
            for n in range(QC):
                disp[i * QC + n, pl.ds(pl.multiple_of(src * unit, unit), unit), :] = rows[
                    unit * n : unit * (n + 1)
                ]

        steps(0, Z // QC, block)

        @pl.when((k > 0) & (lax.rem(k, RING_EVERY) == 0) & (k <= RING_EVERY * early))
        def _():
            ring_step(lax.div(k, RING_EVERY))

    steps(0, G, dispatch_step)

    first_core = (r80 < cap) | ((r80 >= half) & (r80 < half + cap))
    low40 = iota((half, LANES), 1) < 64

    def rs_copy(k, v):
        d = dp(k)
        return rdma(
            sbuf.at[d, pl.ds(v * UG, UG)], rb.at[g, pl.ds(v * UG, UG)],
            s_rs.at[k, v], r_rs.at[g, v], {"dp": d},
        )

    def project_unit(u):
        @pl.when(u + 1 > early)
        def _():
            ring_step(u + 1)

        for par in range(2):
            m = 2 * u + par
            rdma(qb.at[m, 1 - c], qb.at[m, 1 - c], s_qp.at[m], r_qp.at[m], {"expert": mate}).wait_recv()

        def batch(b):
            outs = []
            for par in range(2):
                m = 2 * u + par
                rows = disp[m, pl.ds(pl.multiple_of(b * GB * unit, GB * unit), GB * unit), :]
                x = lax.dot_general(
                    rows, qb[m].reshape(2 * LANES, Dd), NT, preferred_element_type=F32
                )
                picked = []
                for i in range(GB):
                    one = x[unit * i : unit * (i + 1)]
                    sel = jnp.where(first_core, one[:, :LANES], one[:, LANES:])
                    picked.append(jnp.where(low40, sel[:half], sel[half:]))
                outs.append(picked)
            for i in range(GB):
                sbuf[b * GB + i, u] = jnp.concatenate([outs[0][i], outs[1][i]], axis=0).astype(BF16)

        steps(0, G // GB, batch)

        @pl.when(lax.rem(u + 1, UG) == 0)
        def _():
            v = lax.div(u, UG)
            steps(1, G, lambda k: rs_copy(k, v).start())

    steps(0, U, project_unit)

    def z_copy(m, core):
        return rdma(
            zs.at[m, core], pz.at[j], s_z.at[m, core], r_z.at[j],
            {"expert": chip(m) * 2 + core},
        )

    pad = jnp.zeros((LANES - unit, LANES), BF16)
    for v in range(V):

        def add(k, acc):
            src = lax.rem(g + G - k, G)
            rdma(
                rb.at[src, pl.ds(v * UG, UG)], rb.at[src, pl.ds(v * UG, UG)],
                s_rs.at[k, v], r_rs.at[src, v], {"dp": src},
            ).wait_recv()
            return acc + rb[src, pl.ds(v * UG, UG)].astype(F32)

        total = lax.fori_loop(1, G, add, sbuf[g, pl.ds(v * UG, UG)].astype(F32))
        for i in range(UG):
            u = v * UG + i
            rows = jnp.concatenate([total[i].astype(BF16), pad], axis=0)
            spread = jnp.dot(emat[...], rows, preferred_element_type=F32).astype(BF16)
            for b in range(4):
                m, core = 2 * u + b // 2, b % 2
                zs[m, core] = spread[SLOT_ROWS * b : SLOT_ROWS * (b + 1)]
                if m == 0:

                    @pl.when(c == core)
                    def _():
                        pz[j] = spread[SLOT_ROWS * b : SLOT_ROWS * (b + 1)]

                    @pl.when(c != core)
                    def _():
                        z_copy(m, core).start()
                else:
                    z_copy(m, core).start()

    def z_wait(k):
        src = lax.rem(j + k, J)
        rdma(pz.at[src], pz.at[src], s_z.at[0, 0], r_z.at[src], {"expert": src}).wait_recv()

    steps(1, J, z_wait)

    for q in range(U):
        blocks = pz[4 * q : 4 * q + 4].reshape(LANES, LANES)
        p640[unit * q : unit * (q + 1), :] = jnp.dot(
            etmat[...], blocks, preferred_element_type=F32
        ).astype(BF16)
    hcopy.wait()
    turned = p640[...].astype(F32).T.astype(BF16)
    for h in range(2):
        ptp[64 * h : 64 * (h + 1), :] = jnp.dot(
            turned[64 * h : 64 * (h + 1)], hv[h], preferred_element_type=F32
        )

    def p_copy(k):
        d = dp(k)
        return rdma(
            ptp.at[pl.ds(pl.multiple_of(d * R8, R8), R8), :], prb.at[g],
            s_p.at[k], r_p.at[g], {"dp": d},
        )

    def share(at):
        return pfull.at[pl.ds(pl.multiple_of(at * R8, R8), R8), :]

    def pf_copy(k):
        return rdma(share(g), share(g), s_pf.at[k], r_pf.at[g], {"dp": dp(k)})

    steps(1, G, lambda k: p_copy(k).start())

    def add_p(k, acc):
        src = lax.rem(g + G - k, G)
        rdma(prb.at[src], prb.at[src], s_p.at[k], r_p.at[src], {"dp": src}).wait_recv()
        return acc + prb[src]

    own_rows = pl.ds(pl.multiple_of(g * R8, R8), R8)
    pfull[own_rows, :] = lax.fori_loop(1, G, add_p, ptp[own_rows, :])
    steps(1, G, lambda k: pf_copy(k).start())

    def pf_wait(k):
        src = lax.rem(g + G - k, G)
        rdma(share(src), share(src), s_pf.at[k], r_pf.at[src], {"dp": src}).wait_recv()

    steps(1, G, pf_wait)

    full = pfull[...]
    gram = lax.dot_general(
        full, full, NT, precision=lax.Precision.HIGHEST, preferred_element_type=F32
    )
    inverse = whitening(gram)
    btr[...] = jnp.dot(
        inverse, full, precision=lax.Precision.HIGHEST, preferred_element_type=F32
    ).astype(BF16)

    QB = min(4, U)
    rows_m = QB * unit
    low_m = iota((rows_m, LANES), 1) < 64

    def map_block(i):
        at = pl.multiple_of(i * rows_m, rows_m)
        found = [
            lax.dot_general(
                hv[h, pl.ds(at, rows_m), :], btr[...], NT, preferred_element_type=F32
            )
            for h in range(2)
        ]
        rows = jnp.where(low_m, found[0], found[1]).astype(BF16)
        for q in range(QB):
            padded = jnp.concatenate([rows[unit * q : unit * (q + 1)], pad], axis=0)
            spread = jnp.dot(emat[...], padded, preferred_element_type=F32).astype(BF16)
            for b in range(4):
                zs2[(i * QB + q) * 4 + b] = spread[SLOT_ROWS * b : SLOT_ROWS * (b + 1)]

    steps(0, U // QB, map_block)

    def back_index(m):
        if m == Z - 1:
            return m
        return m + 1 if m % 2 else max(m - 1, 0)

    def m_copy(m, core):
        target = chip(m) * 2 + core
        return rdma(
            zs2.at[target], mz.at[back_index(m), c], s_m.at[m, core],
            r_m.at[back_index(m), c], {"expert": target},
        )

    for m in reversed(range(Z)):
        for core in range(2):
            if m == 0:

                @pl.when(c == core)
                def _():
                    mz[0, c] = zs2[j]

                @pl.when(c != core)
                def _():
                    m_copy(0, core).start()
            else:
                m_copy(m, core).start()

    def m_wait(m, core):
        rdma(
            mz.at[m, core], mz.at[m, core], s_m.at[m, core], r_m.at[m, core],
            {"expert": mate},
        ).wait_recv()

    def mg_copy(k, v):
        part = mg.at[g, pl.ds(v * UG, UG)]
        return rdma(part, part, s_mg.at[k, v], r_mg.at[g, v], {"dp": dp(k)})

    for v in reversed(range(V)):
        for u in reversed(range(v * UG, (v + 1) * UG)):
            for b in range(4):
                m, core = 2 * u + b // 2, b % 2
                if m == 0:

                    @pl.when(c != core)
                    def _():
                        m_wait(0, core)
                else:
                    m_wait(m, core)
            blocks = mz[2 * u : 2 * u + 2].reshape(LANES, LANES)
            mg[g, u] = jnp.dot(etmat[...], blocks, preferred_element_type=F32).astype(BF16)
        steps(1, G, lambda k: mg_copy(k, v).start())

    low_core = first_core[:half]
    keep = [
        [low40 & low_core, low40 & jnp.logical_not(low_core)],
        [jnp.logical_not(low40) & low_core, jnp.logical_not(low40) & jnp.logical_not(low_core)],
    ]

    def half_copy(m):
        return rdma(qp.at[m, 1 - c], qh.at[m], s_h.at[m], r_h.at[m], {"expert": mate})

    def up_copy(s):
        return rdma(fs.at[s - 1], fr.at[s - 1], s_f.at[s - 1], r_f.at[s - 1], {"expert": up})

    def down_copy(s):
        return rdma(bs.at[s - 1], br.at[s - 1], s_b.at[s - 1], r_b.at[s - 1], {"expert": down})

    def sum_step(s):
        m = 2 * (U + 1 - s) - 1
        half_copy(m).wait_recv()
        value = qp[m, c] + qh[m]

        @pl.when(s > 1)
        def _():
            up_copy(s - 1).wait_recv()
            fs[s - 1] = value + fr[s - 2]

        @pl.when(s <= 1)
        def _():
            fs[s - 1] = value

        up_copy(s).start()

        @pl.when(s < U)
        def _():
            n = 2 * (U - s)
            half_copy(n).wait_recv()
            other = qp[n, c] + qh[n]

            @pl.when(s > 1)
            def _():
                down_copy(s - 1).wait_recv()
                bs[s - 1] = other + br[s - 2]

            @pl.when(s <= 1)
            def _():
                bs[s - 1] = other

            down_copy(s).start()

    def factor_unit(i):
        u = U - 1 - i

        @pl.when(lax.rem(i, UG) == 0)
        def _():
            v = lax.div(u, UG)

            def wait(k):
                src = lax.rem(g + G - k, G)
                part = mg.at[src, pl.ds(v * UG, UG)]
                rdma(part, part, s_mg.at[k, v], r_mg.at[src, v], {"dp": src}).wait_recv()

            steps(1, G, wait)

        def spread(b):
            rows = mg[b, u].astype(F32)
            for par in range(2):
                one = rows[half * par : half * (par + 1)]
                wide = [
                    jnp.concatenate([jnp.where(keep[h][core], one, 0.0) for h in range(2)], axis=0)
                    for core in range(2)
                ]
                at = pl.ds(pl.multiple_of(b * unit, unit), unit)
                ybuf[par, at, 0:LANES] = wide[0].astype(BF16)
                ybuf[par, at, LANES : 2 * LANES] = wide[1].astype(BF16)

        steps(0, G, spread)
        for par in range(2):
            m = 2 * u + par
            found = lax.dot_general(ybuf[par], disp[m], TN, preferred_element_type=F32)
            qp[m, 0] = found[:LANES]
            qp[m, 1] = found[LANES:]
            half_copy(m).start()

        @pl.when(i > 0)
        def _():
            sum_step(i)

    steps(0, U, factor_unit)
    sum_step(U)
    half_copy(0).wait_recv()
    total = qp[0, c] + qh[0]
    if U > 1:
        down_copy(U - 1).wait_recv()
        total = total + br[U - 2]
    up_copy(U).wait_recv()
    q_out[...] = total + fr[U - 1]

    share_cols = FF // G
    start = g * share_cols
    tile = jnp.minimum(lax.div(start, LANES), FF // LANES - 2)
    window = pfull[:, pl.ds(pl.multiple_of(tile * LANES, LANES), 2 * LANES)]
    shift = lax.rem(3 * LANES + tile * LANES - start - LANES + 2 * LANES, 2 * LANES)
    p_out[...] = pltpu.roll(window, shift, 1)[:, :share_cols]

    def drain_dp(k):
        g_copy(k).wait_send()
        cot_copy(k).wait_send()
        p_copy(k).wait_send()
        pf_copy(k).wait_send()
        for v in range(V):
            rs_copy(k, v).wait_send()
            mg_copy(k, v).wait_send()

    steps(1, G, drain_dp)

    def drain_ring(m):
        ring_copy(qt, m, m, up).wait_send()

    steps(1, Z, drain_ring)

    def drain_mate(m):
        mate_copy(qt, m).wait_send()
        half_copy(m).wait_send()

    steps(0, Z, drain_mate)
    for m in range(Z):
        for core in range(2):
            if m == 0:

                @pl.when(c != core)
                def _():
                    z_copy(0, core).wait_send()
                    m_copy(0, core).wait_send()
            else:
                z_copy(m, core).wait_send()
                m_copy(m, core).wait_send()
    steps(1, U + 1, lambda s: up_copy(s).wait_send())
    steps(1, U, lambda s: down_copy(s).wait_send())


def local(cotangent, expert_ids, gates, hidden, q_prev):
    G, J = lax.axis_size("dp"), lax.axis_size("expert")
    T, width = cotangent.shape
    rows, FF = hidden.shape[2], hidden.shape[3]
    cap = rows // J
    rank = q_prev.shape[2]
    Dd = width // G
    Z, U = J // 2, J // 4
    V = max(1, U // UNIT_GROUP)
    unit = 4 * cap
    qt = jnp.swapaxes(q_prev, 1, 2).reshape(2 * rank, Dd)
    vm, sem = pltpu.VMEM, pltpu.SemaphoreType.DMA
    scratch = [
        vm((G, T, Dd), BF16),
        vm((G, T, LANES), BF16),
        vm((Z * unit, LANES), BF16),
        vm((4 * unit, LANES), F32),
        vm((LANES, LANES), BF16),
        vm((unit, LANES), BF16),
        vm((Z, G * unit, Dd), BF16),
        vm((Z, 2, LANES, Dd), BF16),
        vm((G, U, unit, LANES), BF16),
        vm((G, U, unit, LANES), BF16),
        vm((Z, 2, SLOT_ROWS, LANES), BF16),
        vm((J, SLOT_ROWS, LANES), BF16),
        vm((2, rows, FF), BF16),
        vm((rows, LANES), BF16),
        vm((LANES, FF), F32),
        vm((G, LANES // G, FF), F32),
        vm((LANES, FF), F32),
        vm((LANES, FF), BF16),
        vm((J, SLOT_ROWS, LANES), BF16),
        vm((Z, 2, SLOT_ROWS, LANES), BF16),
        vm((G, U, unit, LANES), BF16),
        vm((2, G * unit, 2 * LANES), BF16),
        vm((Z, 2, LANES, Dd), F32),
        vm((Z, LANES, Dd), F32),
        vm((U, LANES, Dd), F32),
        vm((U, LANES, Dd), F32),
        vm((max(1, U - 1), LANES, Dd), F32),
        vm((max(1, U - 1), LANES, Dd), F32),
        pltpu.SemaphoreType.DMA,
        sem((G,)), sem((G,)), sem((G,)), sem((G,)),
        sem((Z,)), sem((Z,)), sem((Z,)), sem((Z,)),
        sem((G, V)), sem((G, V)),
        sem((Z, 2)), sem((J,)),
        sem((G,)), sem((G,)), sem((G,)), sem((G,)),
        sem((Z, 2)), sem((Z, 2)),
        sem((G, V)), sem((G, V)),
        sem((Z,)), sem((Z,)),
        sem((U,)), sem((U,)), sem((max(1, U - 1),)), sem((max(1, U - 1),)),
    ]
    full = pl.BlockSpec(memory_space=pltpu.VMEM)
    p_t, q_t = pl.pallas_call(
        functools.partial(kernel, (G, J, cap)),
        out_shape=(
            jax.ShapeDtypeStruct((LANES, FF // G), F32),
            jax.ShapeDtypeStruct((LANES, Dd), F32),
        ),
        in_specs=[full, full, full, full, pl.BlockSpec(memory_space=pl.ANY)],
        out_specs=(full, full),
        scratch_shapes=scratch,
        compiler_params=pltpu.CompilerParams(
            collective_id=0, has_side_effects=True, vmem_limit_bytes=60 * 2**20
        ),
    )(cotangent, expert_ids, gates, qt, hidden)
    p_share = jnp.swapaxes(p_t.reshape(2, rank, FF // G), 1, 2)
    q_share = jnp.swapaxes(q_t.reshape(2, rank, Dd), 1, 2)
    return (p_share, q_share)


def solution(mesh):
    placed = (
        P(("dp", "expert"), None),
        P(("dp", "expert"), None),
        P(("dp", "expert"), None),
        P("expert", "dp", None, None),
        P("expert", "dp", None),
    )
    return jax.shard_map(
        local,
        mesh=mesh,
        in_specs=placed,
        out_specs=(P("expert", "dp", None), P("expert", "dp", None)),
        check_vma=False,
    )
```

```python
import functools

import jax
import jax.numpy as jnp
from jax import lax
from jax.experimental import pallas as pl
from jax.experimental.pallas import tpu as pltpu
from jax.sharding import PartitionSpec as P

F32, BF16 = jnp.float32, jnp.bfloat16
MESH = pl.DeviceIdType.MESH
NT = (((1,), (1,)), ((), ()))
TN = (((0,), (0,)), ((), ()))
LANES = 128
SLOT_ROWS = 32
UNIT_GROUP = 2
SIDE = 4
RING_EVERY = 5
RING_FIRST = 4
TABLE_ROWS = 16


def rdma(src, dst, send_sem, recv_sem, device):
    return pltpu.make_async_remote_copy(
        src_ref=src, dst_ref=dst, send_sem=send_sem, recv_sem=recv_sem,
        device_id=device, device_id_type=MESH,
    )


def iota(shape, dim):
    return lax.broadcasted_iota(jnp.int32, shape, dim)


def steps(start, stop, body):
    def run(i, carry):
        body(i)
        return carry

    lax.fori_loop(start, stop, run, 0)


def whitening(gram):
    half = gram.shape[0] // 2
    lane, row = iota((half, LANES), 1), iota((half, LANES), 0)
    low = lane < half
    eye = jnp.where((lane == row) | (lane == row + half), 1.0, 0.0).astype(F32)
    tables = [jnp.where(low, gram[:half], eye), jnp.where(low, eye, gram[half:])]
    blocks = [[t[8 * b : 8 * b + 8] for b in range(half // 8)] for t in tables]
    sub = iota((8, LANES), 0)
    for k in range(half):
        own, at = k // 8, k % 8
        for which in range(2):
            parts = blocks[which]
            pivot_lane = k + which * half
            pivot_row = parts[own][at : at + 1, :]
            scaled = pivot_row / pivot_row[:, pivot_lane : pivot_lane + 1]
            for b in range(own, half // 8):
                column = parts[b][:, pivot_lane : pivot_lane + 1]
                update = column * scaled
                if b == own:
                    update = jnp.where(sub > at, update, 0.0)
                parts[b] = parts[b] - update
    done = [jnp.concatenate(parts, axis=0) for parts in blocks]
    result = []
    for which in range(2):
        diag = jnp.sum(
            jnp.where(lane == row + which * half, done[which], 0.0), axis=1, keepdims=True
        )
        moved = pltpu.roll(done[which] * lax.rsqrt(diag), half, 1)
        result.append(jnp.where(low if which == 0 else jnp.logical_not(low), moved, 0.0))
    return jnp.concatenate(result, axis=0)


def kernel(
    dims,
    cot, ids, gts, qt, hid,
    p_out, q_out,
    cotb, gb, erel, tabg, tabs, emat, etmat, disp, qb, sbuf, rb, zs, pz, hv, p640,
    ptp, prb, pfull, btr, zs2, mz, mg, ybuf, qp, qh, f16s, f16r, f32s, f32r, b16s, b16r, b32s, b32r, work,
    hsem, s_cot, r_cot, s_g, r_g, s_q, r_q, s_qp, r_qp, s_rs, r_rs, s_z, r_z,
    s_p, r_p, s_pf, r_pf, s_m, r_m, s_mg, r_mg, s_h, r_h, s_f, r_f, s_b, r_b,
):
    G, J, cap = dims
    Z, U = J // 2, J // 4
    V = max(1, U // UNIT_GROUP)
    UG = U // V
    T, width = cot.shape
    Dd = width // G
    unit = 4 * cap
    half = 2 * cap
    GB = min(4, G)
    R8 = LANES // G
    FF = hid.shape[-1]
    g = lax.axis_index("dp")
    j = lax.axis_index("expert")
    z, c = lax.div(j, 2), lax.rem(j, 2)
    mate = j + 1 - 2 * c
    up = lax.rem(z + 1, Z) * 2 + c
    down = lax.rem(z + Z - 1, Z) * 2 + c

    def dp(k):
        return lax.rem(g + k, G)

    def chip(m):
        return lax.rem(z + ((m + 1) // 2 if m % 2 else Z - m // 2), Z)

    hcopy = pltpu.make_async_copy(hid.at[:, 0], hv, hsem)
    hcopy.start()

    barrier = pltpu.get_barrier_semaphore()

    def greet_dp(k):
        pl.semaphore_signal(barrier, inc=1, device_id={"dp": dp(k)}, device_id_type=MESH)

    def greet_expert(k):
        pl.semaphore_signal(
            barrier, inc=1, device_id={"expert": lax.rem(j + k, J)}, device_id_type=MESH
        )

    steps(1, G, greet_dp)
    steps(1, J, greet_expert)

    gb[g] = jnp.concatenate([ids[...].astype(F32), gts[...].astype(F32)], axis=0).astype(BF16)

    sub = iota((8, LANES), 0)
    for i in range(Z // 2):
        near = jnp.where(sub < 4, 4 * chip(2 * i), 4 * chip(2 * i + 1) - 4)
        erel[8 * i : 8 * i + 8, :] = (near + sub).astype(F32)
    before = jnp.where(iota((T, T), 0) < iota((T, T), 1), 1.0, 0.0).astype(BF16)
    slot_rows = [
        value.astype(F32)
        for value in (sub, sub + 8, jnp.where(sub < 4, sub + 16, sub - 4), sub + 4, sub + 12)
    ]
    r80, l80 = iota((unit, LANES), 0), iota((unit, LANES), 1)
    er, el = iota((LANES, LANES), 0), iota((LANES, LANES), 1)
    eblk = (
        jnp.where(er >= SLOT_ROWS, 1, 0)
        + jnp.where(er >= 2 * SLOT_ROWS, 1, 0)
        + jnp.where(er >= 3 * SLOT_ROWS, 1, 0)
    )
    inside = er - SLOT_ROWS * eblk
    emat[...] = jnp.where((inside < cap) & (el == inside + cap * eblk), 1.0, 0.0).astype(BF16)
    tblk = (
        jnp.where(r80 >= cap, 1, 0)
        + jnp.where(r80 >= 2 * cap, 1, 0)
        + jnp.where(r80 >= 3 * cap, 1, 0)
    )
    etmat[...] = jnp.where(l80 == r80 + (SLOT_ROWS - cap) * tblk, 1.0, 0.0).astype(BF16)

    pl.semaphore_wait(barrier, G + J - 2)

    def cot_copy(k):
        d = dp(k)
        return rdma(
            cot.at[:, pl.ds(pl.multiple_of(d * Dd, Dd), Dd)], cotb.at[g],
            s_cot.at[k], r_cot.at[g], {"dp": d},
        )

    def g_copy(k):
        return rdma(gb.at[g], gb.at[g], s_g.at[k], r_g.at[g], {"dp": dp(k)})

    def ring_copy(src, m, sem_at, device):
        return rdma(src, qb.at[m, c], s_q.at[sem_at], r_q.at[m], {"expert": device})

    def mate_copy(src, m):
        return rdma(src, qb.at[m, c], s_qp.at[m], r_qp.at[m], {"expert": mate})

    def ring_first():
        ring_copy(qt, 1, 1, down).start()
        if Z > 2:
            ring_copy(qt, 2, 2, up).start()
        mate_copy(qt, 0).start()

    ring_first()

    def send_cot(k):
        g_copy(k).start()
        cot_copy(k).start()

    steps(1, G, send_cot)
    qb[0, c] = qt[...]
    cotb[g] = cot[:, pl.ds(pl.multiple_of(g * Dd, Dd), Dd)]

    def ring_step(s):
        m = 2 * s - 1
        ring_copy(qb.at[m, c], m, m, down).wait_recv()

        @pl.when(s < Z // 2)
        def _():
            ring_copy(qb.at[m, c], m + 2, m + 2, down).start()

        mate_copy(qb.at[m, c], m).start()

        @pl.when(s < Z // 2)
        def _():
            n = 2 * s
            ring_copy(qb.at[n, c], n, n, up).wait_recv()

            @pl.when(s < Z // 2 - 1)
            def _():
                ring_copy(qb.at[n, c], n + 2, n + 2, up).start()

            mate_copy(qb.at[n, c], n).start()

    first_steps = min(RING_FIRST, Z // 2)
    early = min(first_steps + G // RING_EVERY, Z // 2)
    QC = min(4, Z)
    steps(1, first_steps + 1, ring_step)

    def dispatch_step(k):
        src = lax.rem(g + G - k, G)

        @pl.when(k > 0)
        def _():
            rdma(gb.at[src], gb.at[src], s_g.at[k], r_g.at[src], {"dp": src}).wait_recv()
            rdma(cotb.at[src], cotb.at[src], s_cot.at[k], r_cot.at[src], {"dp": src}).wait_recv()

        table = gb[src].astype(F32)
        found = jnp.zeros(tabg.shape, F32)
        wanted = erel[...]
        for n in range(TABLE_ROWS // 2):
            hit = table[n : n + 1, :] == wanted
            found = jnp.where(hit, table[TABLE_ROWS // 2 + n : TABLE_ROWS // 2 + n + 1, :], found)
        tabg[...] = found
        named = jnp.where(found > 0.0, 1.0, 0.0).astype(BF16)
        tabs[...] = jnp.dot(named, before, preferred_element_type=F32)
        tokens = cotb[src]
        at = pl.ds(pl.multiple_of(src * unit, unit), unit)

        def wide(ref, row):
            return jnp.broadcast_to(ref[row : row + 1, :], (8, LANES))

        for m0 in range(0, Z, QC):
            pieces = []
            for m in range(m0, m0 + QC):
                for h in range(2):
                    gate = [wide(tabg, 4 * m + 2 * core + h) for core in range(2)]
                    slot = [wide(tabs, 4 * m + 2 * core + h) for core in range(2)]
                    gates = [gate[0], gate[0], jnp.where(sub < 4, *gate), gate[1], gate[1]]
                    slots = [slot[0], slot[0], jnp.where(sub < 4, *slot), slot[1], slot[1]]
                    for n in range(5):
                        pieces.append(jnp.where(slots[n] == slot_rows[n], gates[n], 0.0))
            chooser = jnp.concatenate(pieces, axis=0).astype(BF16)
            rows = jnp.dot(chooser, tokens, preferred_element_type=F32).astype(BF16)
            for n in range(QC):
                disp[m0 + n, at, :] = rows[unit * n : unit * (n + 1)]

        @pl.when((lax.rem(k, RING_EVERY) == RING_EVERY - 1) & (k < RING_EVERY * (early - first_steps)))
        def _():
            ring_step(first_steps + lax.div(k + 1, RING_EVERY))

    steps(0, G, dispatch_step)

    first_core = (r80 < cap) | ((r80 >= half) & (r80 < half + cap))
    low40 = iota((half, LANES), 1) < 64

    def rs_copy(k, v):
        d = dp(k)
        return rdma(
            sbuf.at[d, pl.ds(v * UG, UG)], rb.at[g, pl.ds(v * UG, UG)],
            s_rs.at[k, v], r_rs.at[g, v], {"dp": d},
        )

    def project_unit(u):
        @pl.when(u + 1 > early)
        def _():
            ring_step(u + 1)

        for par in range(2):
            m = 2 * u + par
            rdma(qb.at[m, 1 - c], qb.at[m, 1 - c], s_qp.at[m], r_qp.at[m], {"expert": mate}).wait_recv()

        def batch(b):
            outs = []
            for par in range(2):
                m = 2 * u + par
                rows = disp[m, pl.ds(pl.multiple_of(b * GB * unit, GB * unit), GB * unit), :]
                x = lax.dot_general(
                    rows, qb[m].reshape(2 * LANES, Dd), NT, preferred_element_type=F32
                )
                picked = []
                for i in range(GB):
                    one = x[unit * i : unit * (i + 1)]
                    sel = jnp.where(first_core, one[:, :LANES], one[:, LANES:])
                    picked.append(jnp.where(low40, sel[:half], sel[half:]))
                outs.append(picked)
            for i in range(GB):
                sbuf[b * GB + i, u] = jnp.concatenate([outs[0][i], outs[1][i]], axis=0).astype(BF16)

        steps(0, G // GB, batch)

        @pl.when(lax.rem(u + 1, UG) == 0)
        def _():
            v = lax.div(u, UG)
            steps(1, G, lambda k: rs_copy(k, v).start())

    steps(0, U, project_unit)

    def z_copy(m, core):
        return rdma(
            zs.at[m, core], pz.at[j], s_z.at[m, core], r_z.at[j],
            {"expert": chip(m) * 2 + core},
        )

    pad = jnp.zeros((LANES - unit, LANES), BF16)
    for v in range(V):

        def add(k, acc):
            src = lax.rem(g + G - k, G)
            rdma(
                rb.at[src, pl.ds(v * UG, UG)], rb.at[src, pl.ds(v * UG, UG)],
                s_rs.at[k, v], r_rs.at[src, v], {"dp": src},
            ).wait_recv()
            return acc + rb[src, pl.ds(v * UG, UG)].astype(F32)

        total = lax.fori_loop(1, G, add, sbuf[g, pl.ds(v * UG, UG)].astype(F32))
        for i in range(UG):
            u = v * UG + i
            rows = jnp.concatenate([total[i].astype(BF16), pad], axis=0)
            spread = jnp.dot(emat[...], rows, preferred_element_type=F32).astype(BF16)
            for b in range(4):
                m, core = 2 * u + b // 2, b % 2
                zs[m, core] = spread[SLOT_ROWS * b : SLOT_ROWS * (b + 1)]
                if m == 0:

                    @pl.when(c == core)
                    def _():
                        pz[j] = spread[SLOT_ROWS * b : SLOT_ROWS * (b + 1)]

                    @pl.when(c != core)
                    def _():
                        z_copy(m, core).start()
                else:
                    z_copy(m, core).start()

    def z_wait(k):
        src = lax.rem(j + k, J)
        rdma(pz.at[src], pz.at[src], s_z.at[0, 0], r_z.at[src], {"expert": src}).wait_recv()

    steps(1, J, z_wait)

    for q in range(U):
        blocks = pz[4 * q : 4 * q + 4].reshape(LANES, LANES)
        p640[unit * q : unit * (q + 1), :] = jnp.dot(
            etmat[...], blocks, preferred_element_type=F32
        ).astype(BF16)
    hcopy.wait()
    turned = p640[...].astype(F32).T.astype(BF16)
    for h in range(2):
        ptp[64 * h : 64 * (h + 1), :] = jnp.dot(
            turned[64 * h : 64 * (h + 1)], hv[h], preferred_element_type=F32
        )

    def p_copy(k):
        d = dp(k)
        return rdma(
            ptp.at[pl.ds(pl.multiple_of(d * R8, R8), R8), :], prb.at[g],
            s_p.at[k], r_p.at[g], {"dp": d},
        )

    def share(at):
        return pfull.at[pl.ds(pl.multiple_of(at * R8, R8), R8), :]

    def pf_copy(k):
        return rdma(share(g), share(g), s_pf.at[k], r_pf.at[g], {"dp": dp(k)})

    steps(1, G, lambda k: p_copy(k).start())

    def add_p(k, acc):
        src = lax.rem(g + G - k, G)
        rdma(prb.at[src], prb.at[src], s_p.at[k], r_p.at[src], {"dp": src}).wait_recv()
        return acc + prb[src]

    own_rows = pl.ds(pl.multiple_of(g * R8, R8), R8)
    pfull[own_rows, :] = lax.fori_loop(1, G, add_p, ptp[own_rows, :])
    steps(1, G, lambda k: pf_copy(k).start())

    def pf_wait(k):
        src = lax.rem(g + G - k, G)
        rdma(share(src), share(src), s_pf.at[k], r_pf.at[src], {"dp": src}).wait_recv()

    steps(1, G, pf_wait)

    full = pfull[...]
    gram = lax.dot_general(
        full, full, NT, precision=lax.Precision.HIGHEST, preferred_element_type=F32
    )
    inverse = whitening(gram)
    btr[...] = jnp.dot(
        inverse, full, precision=lax.Precision.HIGHEST, preferred_element_type=F32
    ).astype(BF16)

    QB = min(4, U)
    rows_m = QB * unit
    low_m = iota((rows_m, LANES), 1) < 64

    def map_block(i):
        at = pl.multiple_of(i * rows_m, rows_m)
        found = [
            lax.dot_general(
                hv[h, pl.ds(at, rows_m), :], btr[...], NT, preferred_element_type=F32
            )
            for h in range(2)
        ]
        rows = jnp.where(low_m, found[0], found[1]).astype(BF16)
        for q in range(QB):
            padded = jnp.concatenate([rows[unit * q : unit * (q + 1)], pad], axis=0)
            spread = jnp.dot(emat[...], padded, preferred_element_type=F32).astype(BF16)
            for b in range(4):
                zs2[(i * QB + q) * 4 + b] = spread[SLOT_ROWS * b : SLOT_ROWS * (b + 1)]

    steps(0, U // QB, map_block)

    def back_index(m):
        if m == Z - 1:
            return m
        return m + 1 if m % 2 else max(m - 1, 0)

    def m_copy(m, core):
        target = chip(m) * 2 + core
        return rdma(
            zs2.at[target], mz.at[back_index(m), c], s_m.at[m, core],
            r_m.at[back_index(m), c], {"expert": target},
        )

    for m in reversed(range(Z)):
        for core in range(2):
            if m == 0:

                @pl.when(c == core)
                def _():
                    mz[0, c] = zs2[j]

                @pl.when(c != core)
                def _():
                    m_copy(0, core).start()
            else:
                m_copy(m, core).start()

    def m_wait(m, core):
        rdma(
            mz.at[m, core], mz.at[m, core], s_m.at[m, core], r_m.at[m, core],
            {"expert": mate},
        ).wait_recv()

    gx, gy = lax.rem(g, SIDE), lax.div(g, SIDE)

    def place(v, da, db):
        flip = lax.rem(v, 2)
        dx = (1 - flip) * da + flip * db
        dy = flip * da + (1 - flip) * db
        return lax.rem(gy + dy, SIDE) * SIDE + lax.rem(gx + dx, SIDE)

    def piece(v, par, da, db, slot, ta, tb):
        part = mg.at[place(v, da, db), 2 * v + par]
        return rdma(
            part, part, s_mg.at[2 * v + par, slot], r_mg.at[place(v, da, db), 2 * v + par],
            {"dp": place(v, ta, tb)},
        )

    def piece_wait(v, par, da, db):
        piece(v, par, da, db, 0, 1, 0).wait_recv()

    def gather_row(v):
        for par in range(2):
            piece(v, par, 0, 0, 0, 1, 0).start()
            piece(v, par, 0, 0, 1, SIDE - 1, 0).start()

    def gather_cross(v):
        for par in range(2):
            piece(v, par, 0, 0, 3, 0, 1).start()
            piece(v, par, 0, 0, 4, 0, SIDE - 1).start()
        for par in range(2):
            for da in (1, SIDE - 1) if par else (SIDE - 1, 1):
                piece_wait(v, par, da, 0)
                if da == (1 if par else SIDE - 1):
                    piece(v, par, da, 0, 2, SIDE - da, 0).start()
                piece(v, par, da, 0, 3 + 2 * da, 0, 1).start()
                piece(v, par, da, 0, 4 + 2 * da, 0, SIDE - 1).start()
        for par in range(2):
            piece_wait(v, par, 2, 0)
            piece(v, par, 2, 0, 3 + 2 * 2, 0, 1).start()
            piece(v, par, 2, 0, 4 + 2 * 2, 0, SIDE - 1).start()

    def gather_far(v):
        def one(da):
            for par in range(2):
                for db in (1, SIDE - 1) if par else (SIDE - 1, 1):
                    piece_wait(v, par, da, db)
                    if db == (1 if par else SIDE - 1):
                        piece(v, par, da, db, 11 + da, 0, SIDE - db).start()

        steps(0, SIDE, one)

    def gather_end(v):
        def one(da):
            for par in range(2):
                piece_wait(v, par, da, 2)

        steps(0, SIDE, one)

    for v in reversed(range(V)):
        for u in reversed(range(v * UG, (v + 1) * UG)):
            for b in range(4):
                m, core = 2 * u + b // 2, b % 2
                if m == 0:

                    @pl.when(c != core)
                    def _():
                        m_wait(0, core)
                else:
                    m_wait(m, core)
            blocks = mz[2 * u : 2 * u + 2].reshape(LANES, LANES)
            mg[g, u] = jnp.dot(etmat[...], blocks, preferred_element_type=F32).astype(BF16)
        gather_row(jnp.int32(v))
    steps(0, V, lambda i: gather_cross(V - 1 - i))
    gather_far(jnp.int32(V - 1))

    low_core = first_core[:half]
    keep = [
        [low40 & low_core, low40 & jnp.logical_not(low_core)],
        [jnp.logical_not(low40) & low_core, jnp.logical_not(low40) & jnp.logical_not(low_core)],
    ]

    def half_copy(m):
        return rdma(qp.at[m, 1 - c], qh.at[m], s_h.at[m], r_h.at[m], {"expert": mate})

    class Chain:
        def __init__(self, near, device, sends, gets, wide_sends, wide_gets, send_sem, get_sem):
            self.near, self.device = near, device
            self.narrow, self.wide = (sends, gets), (wide_sends, wide_gets)
            self.sems = (send_sem, get_sem)

        def copy(self, s, narrow):
            sends, gets = self.narrow if narrow else self.wide
            at = s - 1 if narrow else s - 1 - self.near
            return rdma(
                sends.at[at], gets.at[at], self.sems[0].at[s - 1], self.sems[1].at[s - 1],
                {"expert": self.device},
            )

        def arrived(self, s):
            @pl.when(s <= self.near)
            def _():
                self.copy(s, True).wait_recv()
                work[...] = work[...] + self.narrow[1][s - 1].astype(F32)

            @pl.when(s > self.near)
            def _():
                self.copy(s, False).wait_recv()
                work[...] = work[...] + self.wide[1][s - 1 - self.near]

        def send(self, m, s):
            half_copy(m).wait_recv()
            work[...] = qp[m, c] + qh[m]

            @pl.when(s > 1)
            def _():
                self.arrived(s - 1)

            @pl.when(s <= self.near)
            def _():
                self.narrow[0][s - 1] = work[...].astype(BF16)
                self.copy(s, True).start()

            @pl.when(s > self.near)
            def _():
                self.wide[0][s - 1 - self.near] = work[...]
                self.copy(s, False).start()

    rise = Chain(max(1, U - 2), up, f16s, f16r, f32s, f32r, s_f, r_f)
    fall = Chain(max(1, U - 3), down, b16s, b16r, b32s, b32r, s_b, r_b)

    def sum_step(s):
        rise.send(2 * (U + 1 - s) - 1, s)

        @pl.when(s < U)
        def _():
            fall.send(2 * (U - s), s)

    def factor_unit(i):
        u = U - 1 - i

        @pl.when(lax.rem(i, UG) == 0)
        def _():
            v = lax.div(u, UG)

            @pl.when(v > 0)
            def _():
                gather_far(v - 1)

            gather_end(v)

        def spread(b):
            rows = mg[b, u].astype(F32)
            for par in range(2):
                one = rows[half * par : half * (par + 1)]
                wide = [
                    jnp.concatenate([jnp.where(keep[h][core], one, 0.0) for h in range(2)], axis=0)
                    for core in range(2)
                ]
                at = pl.ds(pl.multiple_of(b * unit, unit), unit)
                ybuf[par, at, 0:LANES] = wide[0].astype(BF16)
                ybuf[par, at, LANES : 2 * LANES] = wide[1].astype(BF16)

        steps(0, G, spread)
        for par in range(2):
            m = 2 * u + par
            found = lax.dot_general(ybuf[par], disp[m], TN, preferred_element_type=F32)
            qp[m, 0] = found[:LANES]
            qp[m, 1] = found[LANES:]
            half_copy(m).start()

        @pl.when(i > 0)
        def _():
            sum_step(i)

    steps(0, U, factor_unit)
    sum_step(jnp.int32(U))
    half_copy(0).wait_recv()
    work[...] = qp[0, c] + qh[0]
    if U > 1:
        fall.arrived(jnp.int32(U - 1))
    rise.arrived(jnp.int32(U))
    q_out[...] = work[...]

    share_cols = FF // G
    start = g * share_cols
    tile = jnp.minimum(lax.div(start, LANES), FF // LANES - 2)
    window = pfull[:, pl.ds(pl.multiple_of(tile * LANES, LANES), 2 * LANES)]
    shift = lax.rem(3 * LANES + tile * LANES - start - LANES + 2 * LANES, 2 * LANES)
    p_out[...] = pltpu.roll(window, shift, 1)[:, :share_cols]

    def drain_dp(k):
        g_copy(k).wait_send()
        cot_copy(k).wait_send()
        p_copy(k).wait_send()
        pf_copy(k).wait_send()
        for v in range(V):
            rs_copy(k, v).wait_send()

    steps(1, G, drain_dp)

    def drain_ring(m):
        ring_copy(qt, m, m, up).wait_send()

    steps(1, Z, drain_ring)

    def drain_mate(m):
        mate_copy(qt, m).wait_send()
        half_copy(m).wait_send()

    steps(0, Z, drain_mate)
    for m in range(Z):
        for core in range(2):
            if m == 0:

                @pl.when(c != core)
                def _():
                    z_copy(0, core).wait_send()
                    m_copy(0, core).wait_send()
            else:
                z_copy(m, core).wait_send()
                m_copy(m, core).wait_send()
    for s in range(1, U + 1):
        rise.copy(s, s <= rise.near).wait_send()
    for s in range(1, U):
        fall.copy(s, s <= fall.near).wait_send()

    def drain_gather(u):
        for slot in range(15):
            rdma(mg.at[g, u], mg.at[g, u], s_mg.at[u, slot], r_mg.at[g, u], {"dp": dp(1)}).wait_send()

    steps(0, U, drain_gather)


def local(cotangent, expert_ids, gates, hidden, q_prev):
    G, J = lax.axis_size("dp"), lax.axis_size("expert")
    T, width = cotangent.shape
    rows, FF = hidden.shape[2], hidden.shape[3]
    cap = rows // J
    rank = q_prev.shape[2]
    Dd = width // G
    Z, U = J // 2, J // 4
    V = max(1, U // UNIT_GROUP)
    unit = 4 * cap
    spare = ((0, TABLE_ROWS // 2 - expert_ids.shape[1]), (0, 0))
    ids = jnp.pad(expert_ids.T, spare, constant_values=-1)
    gts = jnp.pad(gates.T, spare)
    qt = jnp.swapaxes(q_prev, 1, 2).reshape(2 * rank, Dd)
    near = (max(1, U - 2), max(1, U - 3))
    sums = [
        (n, kind)
        for n, kind in (
            (near[0], BF16), (near[0], BF16), (U - near[0], F32), (U - near[0], F32),
            (near[1], BF16), (near[1], BF16), (U - 1 - near[1], F32), (U - 1 - near[1], F32),
        )
    ]
    vm, sem = pltpu.VMEM, pltpu.SemaphoreType.DMA
    scratch = [
        vm((G, T, Dd), BF16),
        vm((G, TABLE_ROWS, LANES), BF16),
        vm((4 * Z, LANES), F32),
        vm((4 * Z, LANES), F32),
        vm((4 * Z, LANES), F32),
        vm((LANES, LANES), BF16),
        vm((unit, LANES), BF16),
        vm((Z, G * unit, Dd), BF16),
        vm((Z, 2, LANES, Dd), BF16),
        vm((G, U, unit, LANES), BF16),
        vm((G, U, unit, LANES), BF16),
        vm((Z, 2, SLOT_ROWS, LANES), BF16),
        vm((J, SLOT_ROWS, LANES), BF16),
        vm((2, rows, FF), BF16),
        vm((rows, LANES), BF16),
        vm((LANES, FF), F32),
        vm((G, LANES // G, FF), F32),
        vm((LANES, FF), F32),
        vm((LANES, FF), BF16),
        vm((J, SLOT_ROWS, LANES), BF16),
        vm((Z, 2, SLOT_ROWS, LANES), BF16),
        vm((G, U, unit, LANES), BF16),
        vm((2, G * unit, 2 * LANES), BF16),
        vm((Z, 2, LANES, Dd), F32),
        vm((Z, LANES, Dd), F32),
        *[vm((max(1, n), LANES, Dd), kind) for n, kind in sums],
        vm((LANES, Dd), F32),
        pltpu.SemaphoreType.DMA,
        sem((G,)), sem((G,)), sem((G,)), sem((G,)),
        sem((Z,)), sem((Z,)), sem((Z,)), sem((Z,)),
        sem((G, V)), sem((G, V)),
        sem((Z, 2)), sem((J,)),
        sem((G,)), sem((G,)), sem((G,)), sem((G,)),
        sem((Z, 2)), sem((Z, 2)),
        sem((U, 15)), sem((G, U)),
        sem((Z,)), sem((Z,)),
        sem((U,)), sem((U,)), sem((max(1, U - 1),)), sem((max(1, U - 1),)),
    ]
    full = pl.BlockSpec(memory_space=pltpu.VMEM)
    p_t, q_t = pl.pallas_call(
        functools.partial(kernel, (G, J, cap)),
        out_shape=(
            jax.ShapeDtypeStruct((LANES, FF // G), F32),
            jax.ShapeDtypeStruct((LANES, Dd), F32),
        ),
        in_specs=[full, full, full, full, pl.BlockSpec(memory_space=pl.ANY)],
        out_specs=(full, full),
        scratch_shapes=scratch,
        compiler_params=pltpu.CompilerParams(
            collective_id=0, has_side_effects=True, vmem_limit_bytes=60 * 2**20
        ),
    )(cotangent, ids, gts, qt, hidden)
    p_share = jnp.swapaxes(p_t.reshape(2, rank, FF // G), 1, 2)
    q_share = jnp.swapaxes(q_t.reshape(2, rank, Dd), 1, 2)
    return (p_share, q_share)


def solution(mesh):
    placed = (
        P(("dp", "expert"), None),
        P(("dp", "expert"), None),
        P(("dp", "expert"), None),
        P("expert", "dp", None, None),
        P("expert", "dp", None),
    )
    return jax.shard_map(
        local,
        mesh=mesh,
        in_specs=placed,
        out_specs=(P("expert", "dp", None), P("expert", "dp", None)),
        check_vma=False,
    )
```
